128 devices in a mesh: inst: 4 (over x_hi, core), space: 32 (over y, z, x_lo).
Axes of the slice: x: 4 (x_hi: 2, x_lo: 2; x = x_hi * 2 + x_lo), y: 4, z: 4, core: 2. Of those that a mesh axis runs over, the one named last changes fastest.
Arguments:
- adjoint: bfloat16 [8, 5, 512, 32, 256], P('inst', None, 'space'), may hold values from -6 to 6
- flux_terms: bfloat16 [8, 5, 3, 512, 32, 256], P('inst', None, None, 'space'), may hold values from -6 to 6
- stiffness: float32 [512, 32, 256], P('space', 'inst'), may hold values from 0.1 to 1
- normals: float32 [3, 512, 32], P(None, 'space', 'inst'), may hold values from -6 to 6
- design_map: int32 [512, 32], P('space', 'inst'), may hold values from 0 to 1023
Outputs:
- mesh_adjoint: float32 [3, 512, 32, 256], P(None, 'space', 'inst')
- design_grad: float32 [1024], P(('inst', 'space'))
The draws below stay inside these ranges and needn't reach their ends.
All inputs are finite; a program needn't handle non-finite values.
Results may differ from the reference program's by a relative error of at most 0.00075.
Values sent between devices are 32-bit elements; how exact they have to be, the bound alone decides.
A program may use at most 64 MiB of HBM per device.

```python
import math
import jax
import jax.numpy as jnp
from jax import lax

NV = 5
NZ = 256
SWEEPS = 2
INSTANCES = 8
NXG = 512
NYG = 32
NDV = 1024


def plant(entries, stream_key, smallest, largest):
    shape = entries.shape
    place = [jax.random.randint(jax.random.fold_in(stream_key, axis), (), 0, shape[axis]) for axis in range(len(shape))]
    entries = entries.at[tuple(place)].set(smallest)
    longest = shape.index(max(shape))
    place[longest] = (place[longest] + 1) % shape[longest]
    return entries.at[tuple(place)].set(largest)


def block_scale(key, dims, pieces, smallest, largest):
    loudness = 1.0
    for position, blocks in pieces:
        heights = jax.random.uniform(jax.random.fold_in(jax.random.fold_in(key, 6), position), (blocks,), jnp.float32, smallest / len(pieces), largest / len(pieces))
        loudness = loudness * jnp.repeat(jnp.exp(heights), dims[position] // blocks).reshape((-1,) + (1,) * (len(dims) - 1 - position))
    return loudness


def noise(own_key, shape, scale, most, split=(), kind=jnp.bfloat16):
    values = jax.random.normal(own_key, shape, jnp.float32) * scale
    if len(split) > 0:
        values = block_scale(own_key, shape, split, -0.22, 0.18) * values
    return jnp.clip(values, min=-most, max=most).astype(kind)


def setup_inputs(seed: int = 0) -> dict:
    arg_keys = jax.random.split(jax.random.key(seed), 6)
    adjoint = noise(arg_keys[0], (INSTANCES, NV, NXG, NYG, NZ), 1.0, 6.0, ((0, 4), (2, 32)))
    flux_terms = noise(arg_keys[1], (INSTANCES, NV, 3, NXG, NYG, NZ), 1.0, 6.0, ((0, 4), (3, 32)))
    stiffness = jnp.clip(jnp.exp(math.log(1.0) - 2.3025851 * jax.random.uniform(arg_keys[2], (NXG, NYG, NZ), jnp.float32) ** block_scale(arg_keys[2], (NXG, NYG, NZ), ((0, 32), (1, 4)), -0.2, 0.2)), 0.1, 1.0)
    normals = noise(arg_keys[3], (3, NXG, NYG), 1.0, 6.0, ((1, 32), (2, 4)), jnp.float32)
    design_map = plant(jax.random.randint(arg_keys[4], (NXG, NYG), 0, NDV), jax.random.fold_in(arg_keys[4], 1), 0, NDV - 1).astype(jnp.int32)
    return {"adjoint": adjoint, "flux_terms": flux_terms, "stiffness": stiffness, "normals": normals, "design_map": design_map}


def transpose_metric(weighted):
    padded = jnp.pad(weighted, ((0, 0), (1, 1), (1, 1), (1, 1)))
    first = padded[0, :-2, 1:-1, 1:-1] - padded[0, 2:, 1:-1, 1:-1]
    second = padded[1, 1:-1, :-2, 1:-1] - padded[1, 1:-1, 2:, 1:-1]
    third = padded[2, 1:-1, 1:-1, :-2] - padded[2, 1:-1, 1:-1, 2:]
    return weighted + 0.5 * jnp.stack([first, second, third])


def neighbours(field):
    padded = jnp.pad(field, ((0, 0), (1, 1), (1, 1), (1, 1)))
    summed = padded[:, :-2, 1:-1, 1:-1] + padded[:, 2:, 1:-1, 1:-1]
    summed = summed + padded[:, 1:-1, :-2, 1:-1] + padded[:, 1:-1, 2:, 1:-1]
    summed = summed + padded[:, 1:-1, 1:-1, :-2] + padded[:, 1:-1, 1:-1, 2:]
    return summed


def reference(adjoint, flux_terms, stiffness, normals, design_map):
    def accumulate(carried, pair):
        adj_one, flux_one = pair
        term = jnp.einsum("vxyz,vdxyz->dxyz", adj_one.astype(jnp.float32), flux_one.astype(jnp.float32))
        return carried + term, None

    start_sum = jnp.zeros((3, NXG, NYG, NZ), jnp.float32)
    summed, _ = lax.scan(accumulate, start_sum, (adjoint, flux_terms))
    weighted = summed / INSTANCES
    volume_grad = transpose_metric(weighted)
    diagonal = 6.5 * stiffness
    mesh_adjoint = volume_grad / diagonal
    for sweep_index in range(SWEEPS):
        mesh_adjoint = (volume_grad + neighbours(stiffness * mesh_adjoint)) / diagonal
    surface = jnp.sum(normals * mesh_adjoint[:, :, :, 0], axis=0)
    flat_ids = design_map.reshape(-1)
    one_hot = (flat_ids[:, None] == jnp.arange(NDV, dtype=jnp.int32)[None, :]).astype(jnp.float32)
    design_grad = jnp.dot(surface.reshape(-1), one_hot, precision=lax.Precision.HIGHEST)
    return mesh_adjoint, design_grad
```

```python
import functools

import jax
import jax.numpy as jnp
from jax import lax
from jax.experimental import pallas as pl
from jax.experimental.pallas import tpu as pltpu
from jax.sharding import PartitionSpec as P

F32 = jnp.float32
MESH = pl.DeviceIdType.MESH
A = 1.0 / 6.5
ROWS = 4
STARTS = (0, 12, 4, 8)
CHUNKS = tuple((zh, x0) for zh in range(2) for x0 in STARTS)
LAG = 3
YZ = 16


def iota(shape, axis):
    return lax.broadcasted_iota(jnp.int32, shape, axis)


def roll(value, shift, axis):
    return pltpu.roll(value, shift % value.shape[axis], axis)


def kernel(
    adj, flux, stiff, normals, dmap, lam_ref, dg_ref,
    av, fv, kv, nv, dv, q, rc, g, xr, ps, pr, w, vg, m1, dsum, ra, rb,
    load_sem, small_sem, c_send, c_recv, x_send, x_recv, h_send, h_recv,
    p_send, p_recv, n_send, n_recv, a_send, a_recv, b_send, b_recv,
):
    inst = lax.axis_index("inst")
    s = lax.axis_index("space")
    h = inst // 2
    c = lax.rem(inst, 2)
    xlo = lax.rem(s, 2)
    yz = s // 2
    partner = (2 * h + 1 - c, s)
    opposite = (2 * (1 - h) + c, s)
    up_dev = (inst, lax.rem(s + 1, 32))
    down_dev = (inst, lax.rem(s + 31, 32))
    has_up = s < 31
    has_down = s > 0
    sends_halo = c == h
    sub = iota((8, 128), 0)
    lane = iota((8, 128), 1)
    zero = jnp.zeros((8, 128), F32)

    loads = []
    for t, (zh, x0) in enumerate(CHUNKS):
        rows, zs = pl.ds(x0, ROWS), pl.ds(zh * 128, 128)
        pair = [
            pltpu.make_async_copy(
                adj.at[:, :, rows, :, zs], av.at[zh, :, :, rows], load_sem.at[t, 0]
            ),
            pltpu.make_async_copy(
                flux.at[:, :, :, rows, :, zs], fv.at[zh, :, :, :, rows], load_sem.at[t, 1]
            ),
        ]
        for copy in pair:
            copy.start()
        loads.append(pair)
    small = [
        pltpu.make_async_copy(stiff, kv, small_sem.at[0]),
        pltpu.make_async_copy(normals, nv, small_sem.at[1]),
        pltpu.make_async_copy(dmap, dv, small_sem.at[2]),
    ]
    for copy in small:
        copy.start()

    def clear(x, _):
        for zh in range(2):
            xr[zh, x, 3] = zero
        return 0

    lax.fori_loop(0, 16, clear, 0)
    for zh in range(2):
        for row in (0, 1, 2, 19, 20, 21):
            for tile in range(6):
                w[zh, row, tile] = zero

    barrier = pltpu.get_barrier_semaphore()

    def signal_yz(j, _):
        target = (inst, lax.rem(yz + j, YZ) * 2 + xlo)
        pl.semaphore_signal(barrier, inc=1, device_id=target, device_id_type=MESH)
        return 0

    lax.fori_loop(1, YZ, signal_yz, 0)
    mine = inst * 2 + xlo

    def x_peer(j):
        other = lax.rem(mine + j, 8)
        return (other // 2, yz * 2 + lax.rem(other, 2))

    for j in range(1, 8):
        pl.semaphore_signal(barrier, inc=1, device_id=x_peer(j), device_id_type=MESH)

    @pl.when(has_up)
    def _():
        pl.semaphore_signal(barrier, inc=1, device_id=up_dev, device_id_type=MESH)

    @pl.when(has_down)
    def _():
        pl.semaphore_signal(barrier, inc=1, device_id=down_dev, device_id_type=MESH)

    def remote(src, dst, send, recv, device):
        return pltpu.make_async_remote_copy(
            src_ref=src, dst_ref=dst, send_sem=send, recv_sem=recv,
            device_id=device, device_id_type=MESH,
        )

    def pack_up(w0, w1, w2):
        return jnp.where(sub < 2, w0, jnp.where(sub < 4, roll(w2, 2, 0), roll(w1, 4, 0)))

    def pack_low(w0, w1, w2):
        return jnp.where(sub >= 6, w0, jnp.where(sub >= 4, roll(w2, 6, 0), roll(w1, 4, 0)))

    def slot(block, core):
        rb = block + h - 2 * block * h
        rk = core + c - 2 * core * c
        return rk * 3 * rb + (1 - rk) * (11 - 4 * rb)

    def core_copy(t):
        zh, x0 = CHUNKS[t]
        rows = pl.ds(x0, ROWS)
        return remote(
            q.at[zh, rows, pl.ds(0, 7)], rc.at[zh, rows], c_send.at[t], c_recv.at[t], partner
        )

    def cross_copy(t):
        zh, x0 = CHUNKS[t]
        rows = pl.ds(x0, ROWS)
        main = pl.ds(0, 3)
        return remote(
            g.at[zh, rows, main], xr.at[zh, rows, main], x_send.at[t], x_recv.at[t], opposite
        )

    def halo_copy(t):
        zh, x0 = CHUNKS[t]
        rows = pl.ds(x0, ROWS)
        last = pl.ds(3, 1)
        return remote(
            g.at[zh, rows, last], xr.at[zh, rows, last], h_send.at[t], h_recv.at[t], opposite
        )

    def pair_copy(t):
        zh, x0 = CHUNKS[t]
        rows = pl.ds(x0, ROWS)
        return remote(ps.at[zh, rows], pr.at[zh, rows], p_send.at[t], p_recv.at[t], partner)

    def partial(t):
        zh, x0 = CHUNKS[t]
        for copy in loads[t]:
            copy.wait()

        def row(r, _):
            x = x0 + r
            tiles = {}
            for block in range(2):
                ys = pl.ds(16 * block, 16)
                acc = [None] * 3
                for k in range(2):
                    for v in range(5):
                        a = av[zh, k, v, x, ys, :].astype(F32)
                        for d in range(3):
                            term = a * fv[zh, k, v, d, x, ys, :].astype(F32)
                            acc[d] = term if acc[d] is None else acc[d] + term
                for core in range(2):
                    base = slot(block, core)
                    for d in range(3):
                        tile = acc[d][8 * core : 8 * core + 8]
                        tiles[block, core, d] = tile
                        q[zh, x, base + d] = tile
            q[zh, x, 6 + 4 * c] = pack_up(*[tiles[1, 0, d] for d in range(3)])
            q[zh, x, 10 - 4 * c] = pack_low(*[tiles[0, 1, d] for d in range(3)])
            return 0

        lax.fori_loop(0, ROWS, row, 0)
        if t == 0:
            extra = has_up.astype(jnp.int32) + has_down.astype(jnp.int32)
            pl.semaphore_wait(barrier, YZ - 1 + 7 + extra)
        core_copy(t).start()

    def cross(t):
        zh, x0 = CHUNKS[t]
        core_copy(t).wait_recv()

        def row(r, _):
            x = x0 + r
            for d in range(4):
                g[zh, x, d] = q[zh, x, 7 + d] + rc[zh, x, 3 + d]
            return 0

        lax.fori_loop(0, ROWS, row, 0)
        cross_copy(t).start()

        @pl.when(sends_halo)
        def _():
            halo_copy(t).start()

    def finish(t):
        zh, x0 = CHUNKS[t]
        cross_copy(t).wait_recv()

        def row(r, _):
            x = x0 + r
            own = [q[zh, x, 11 + d] + rc[zh, x, d] + xr[zh, x, d] for d in range(3)]
            w[zh, x + 3, 0] = own[0]
            w[zh, x + 3, 2] = own[1]
            w[zh, x + 3, 3] = own[2]
            ps[zh, x] = jnp.where(c == 0, pack_low(*own), pack_up(*own))
            return 0

        lax.fori_loop(0, ROWS, row, 0)
        pair_copy(t).start()

    def halo(t):
        zh, x0 = CHUNKS[t]
        pair_copy(t).wait_recv()

        @pl.when(jnp.logical_not(sends_halo))
        def _():
            halo_copy(t).wait_recv()

        def row(r, _):
            x = x0 + r
            far = jnp.where(sends_halo, zero, g[zh, x, 3] + xr[zh, x, 3])
            near = pr[zh, x]
            top = jnp.where(c == 0, near, far)
            low = jnp.where(c == 0, far, near)
            w[zh, x + 3, 1] = jnp.where(sub < 2, top, jnp.where(sub >= 6, low, 0.0))
            w[zh, x + 3, 4] = jnp.where(
                sub < 3, roll(top, 4, 0), jnp.where(sub >= 5, roll(low, 4, 0), 0.0)
            )
            w[zh, x + 3, 5] = jnp.where(
                sub < 2, roll(top, 6, 0), jnp.where(sub >= 6, roll(low, 2, 0), 0.0)
            )
            return 0

        lax.fori_loop(0, ROWS, row, 0)

    def side_copies(zh, side):
        out = []
        for j, width in enumerate((6, 5, 1)):
            src = 18 - j if side == 0 else 3 + j
            dst = 2 - j if side == 0 else 19 + j
            tiles = pl.ds(0, width)
            out.append(
                remote(
                    w.at[zh, src, tiles], w.at[zh, dst, tiles],
                    n_send.at[zh, side, j], n_recv.at[zh, side, j],
                    up_dev if side == 0 else down_dev,
                )
            )
        return out

    def side_send(zh):
        for side, there in ((0, has_up), (1, has_down)):
            @pl.when(there)
            def _(side=side):
                for copy in side_copies(zh, side):
                    copy.start()

    def side_wait(zh):
        for side, there in ((0, has_down), (1, has_up)):
            @pl.when(there)
            def _(side=side):
                for copy in side_copies(zh, side):
                    copy.wait_recv()

    up_ok = (inst < 3).astype(F32)
    low_ok = (inst > 0).astype(F32)
    ring_mask = jnp.where(sub < 4, up_ok, low_ok)
    x_low_ok = has_down.astype(F32)
    x_up_ok = has_up.astype(F32)

    def x_mask(row):
        return jnp.where(row < 3, x_low_ok, jnp.where(row > 18, x_up_ok, 1.0))

    def y_before(own, ring):
        a, b = roll(own, 1, 0), roll(ring, 1, 0)
        return jnp.where(sub == 0, b, a), jnp.where(sub == 0, a, b)

    def y_after(own, ring):
        a, b = roll(own, 7, 0), roll(ring, 7, 0)
        return jnp.where(sub == 7, b, a), jnp.where(sub == 7, a, b)

    def z_before(parts):
        turned = [roll(p, 1, 1) for p in parts]
        return [
            jnp.where(lane == 0, turned[z - 1] if z else 0.0, turned[z]) for z in range(len(parts))
        ]

    def z_after(parts):
        turned = [roll(p, 127, 1) for p in parts]
        last = len(parts) - 1
        return [
            jnp.where(lane == 127, turned[z + 1] if z < last else 0.0, turned[z])
            for z in range(len(parts))
        ]

    own_at = (0, 2, 3)
    ring_at = (1, 4, 5)

    def gradient(halves):
        zs = range(halves)

        def row(x, _):
            xm = x_mask(x)
            rm = ring_mask * xm
            for tile, at in ((0, own_at), (1, ring_at)):
                m = xm if tile == 0 else rm
                for z in zs:
                    mid = w[z, x, at[0]]
                    diff = w[z, x - 1, at[0]] - w[z, x + 1, at[0]]
                    vg[z, x, 0, tile] = (mid + 0.5 * diff) * m
                parts = [w[z, x, at[2]] for z in zs]
                before, after = z_before(parts), z_after(parts)
                for z in zs:
                    vg[z, x, 2, tile] = (parts[z] + 0.5 * (before[z] - after[z])) * m
            for z in zs:
                own, ring = w[z, x, own_at[1]], w[z, x, ring_at[1]]
                before, after = y_before(own, ring), y_after(own, ring)
                vg[z, x, 1, 0] = (own + 0.5 * (before[0] - after[0])) * xm
                vg[z, x, 1, 1] = (ring + 0.5 * (before[1] - after[1])) * rm
            return 0

        lax.fori_loop(1, 21, row, 0)

    def around(ref, x, d, zs, tiles):
        own = [ref[z, x, d, 0] for z in zs]
        ring = [ref[z, x, d, 1] for z in zs]
        total = {}
        for z in zs:
            before, after = y_before(own[z], ring[z]), y_after(own[z], ring[z])
            for tile in tiles:
                total[z, tile] = (
                    before[tile] + after[tile] + ref[z, x - 1, d, tile] + ref[z, x + 1, d, tile]
                )
        for tile in tiles:
            parts = own if tile == 0 else ring
            before, after = z_before(parts), z_after(parts)
            for z in zs:
                total[z, tile] = total[z, tile] + before[z] + after[z]
        return total

    def sweep(halves):
        zs = range(halves)

        def row(x, _):
            xm = x_mask(x) * A
            rm = ring_mask * xm
            for d in range(3):
                total = around(vg, x, d, zs, (0, 1))
                for z in zs:
                    m1[z, x, d, 0] = (vg[z, x, d, 0] + A * total[z, 0]) * xm
                    m1[z, x, d, 1] = (vg[z, x, d, 1] + A * total[z, 1]) * rm
            return 0

        lax.fori_loop(2, 20, row, 0)

    def last_sweep(x, halves):
        zs = range(halves)
        out = [[None] * 3 for _ in zs]
        for z in zs:
            out[z] = [None] * 3
        scale = [0.125 / (6.5 * kv[x, :, 128 * z : 128 * z + 128]) for z in zs]
        for d in range(3):
            total = around(m1, x + 3, d, zs, (0,))
            for z in zs:
                out[z][d] = (vg[z, x + 3, d, 0] + total[z, 0]) * scale[z]
        return out

    def yz_copy(j):
        target = (inst, lax.rem(yz + j, YZ) * 2 + xlo)
        return remote(dsum.at[0], ra.at[j], a_send.at[j], a_recv.at[j], target)

    def x_copy(j):
        return remote(dsum.at[1], rb.at[j], b_send.at[j], b_recv.at[j], x_peer(j))

    def design_start():
        gradient(1)
        sweep(1)
        small[0].wait()

        def row(x, wall):
            lam = last_sweep(x, 1)[0]
            return tuple(
                jnp.where(lane == x, jnp.broadcast_to(lam[d][:, 0:1], (8, 128)), wall[d])
                for d in range(3)
            )

        wall = lax.fori_loop(0, 16, row, (zero, zero, zero))
        small[1].wait()
        small[2].wait()
        surface = sum(nv[d] * wall[d][:, :16] for d in range(3))
        ids = dv[...]
        values = jnp.concatenate([surface[y : y + 1, :] for y in range(8)], axis=1)
        flat = jnp.concatenate([ids[y : y + 1, :] for y in range(8)], axis=1)
        high, low = flat // 128, lax.rem(flat, 128)
        left = jnp.where(
            jnp.broadcast_to(high, (8, 128)) == sub, jnp.broadcast_to(values, (8, 128)), 0.0
        )
        right = (jnp.broadcast_to(low, (128, 128)) == iota((128, 128), 0)).astype(F32)
        dsum[0] = lax.dot_general(
            left, right, (((1,), (1,)), ((), ())),
            precision=lax.Precision.HIGHEST, preferred_element_type=F32,
        )

        def send(j, _):
            yz_copy(j).start()
            return 0

        lax.fori_loop(1, YZ, send, 0)

    def design_middle():
        def take(j, total):
            yz_copy(j).wait_recv()
            return total + ra[j]

        dsum[1] = lax.fori_loop(1, YZ, take, dsum[0])
        for j in range(1, 8):
            x_copy(j).start()

    def design_end():
        total = dsum[1]
        for j in range(1, 8):
            x_copy(j).wait_recv()
            total = total + rb[j]
        device = inst * 32 + s
        picked = jnp.where(sub == device // 16, total, 0.0)
        line = jnp.broadcast_to(jnp.sum(picked, axis=0, keepdims=True), (8, 128))
        turned = pltpu.roll(line, lax.rem(128 - lax.rem(device, 16) * 8, 128), 1)
        dg_ref[...] = turned[0:1, :8]

    count = len(CHUNKS)
    for t in range(count + LAG + 3):
        if t < count:
            partial(t)
        if 0 <= t - 1 < count:
            cross(t - 1)
        if 0 <= t - 1 - LAG < count:
            finish(t - 1 - LAG)
        done = t - 2 - LAG
        if 0 <= done < count:
            halo(done)
            if done % 4 == 1:
                side_send(done // 4)
            if done == 3:
                side_wait(0)
                design_start()
            if done == 6:
                design_middle()
    side_wait(1)
    gradient(2)
    sweep(2)

    def emit(x, _):
        lam = last_sweep(x, 2)
        for z in range(2):
            for d in range(3):
                lam_ref[d, x, :, 128 * z : 128 * z + 128] = lam[z][d]
        return 0

    lax.fori_loop(0, 16, emit, 0)
    design_end()

    for t in range(count):
        core_copy(t).wait_send()
        cross_copy(t).wait_send()
        pair_copy(t).wait_send()

    @pl.when(sends_halo)
    def _():
        for t in range(count):
            halo_copy(t).wait_send()

    for zh in range(2):
        for side, there in ((0, has_up), (1, has_down)):
            @pl.when(there)
            def _(zh=zh, side=side):
                for copy in side_copies(zh, side):
                    copy.wait_send()

    def drain(j, _):
        yz_copy(j).wait_send()
        return 0

    lax.fori_loop(1, YZ, drain, 0)
    for j in range(1, 8):
        x_copy(j).wait_send()


def per_device(adjoint, flux_terms, stiffness, normals, design_map):
    hbm = pl.BlockSpec(memory_space=pl.ANY)
    dma = pltpu.SemaphoreType.DMA
    count = len(CHUNKS)

    def tiles(*lead):
        return pltpu.VMEM(lead + (8, 128), F32)

    lam, grad = pl.pallas_call(
        kernel,
        out_shape=(
            jax.ShapeDtypeStruct((3, 16, 8, 256), F32),
            jax.ShapeDtypeStruct((1, 8), F32),
        ),
        in_specs=[hbm] * 5,
        out_specs=(
            pl.BlockSpec(memory_space=pltpu.VMEM),
            pl.BlockSpec(memory_space=pltpu.VMEM),
        ),
        scratch_shapes=[
            pltpu.VMEM((2, 2, 5, 16, 32, 128), jnp.bfloat16),
            pltpu.VMEM((2, 2, 5, 3, 16, 32, 128), jnp.bfloat16),
            pltpu.VMEM((16, 8, 256), F32),
            pltpu.VMEM((3, 8, 16), F32),
            pltpu.VMEM((8, 16), jnp.int32),
            tiles(2, 16, 14),
            tiles(2, 16, 7),
            tiles(2, 16, 4),
            tiles(2, 16, 4),
            tiles(2, 16),
            tiles(2, 16),
            tiles(2, 22, 6),
            tiles(2, 22, 3, 2),
            tiles(2, 22, 3, 2),
            tiles(2),
            tiles(YZ),
            tiles(8),
            dma((count, 2)),
            dma((3,)),
            dma((count,)), dma((count,)), dma((count,)), dma((count,)),
            dma((count,)), dma((count,)), dma((count,)), dma((count,)),
            dma((2, 2, 3)), dma((2, 2, 3)),
            dma((YZ,)), dma((YZ,)), dma((8,)), dma((8,)),
        ],
        compiler_params=pltpu.CompilerParams(
            collective_id=0, has_side_effects=True, vmem_limit_bytes=60 * 1024 * 1024
        ),
    )(adjoint, flux_terms, stiffness, normals.transpose(0, 2, 1), design_map.T)
    return lam, grad.reshape(8)


def solution(mesh):
    in_specs = (
        P("inst", None, "space", None, None),
        P("inst", None, None, "space", None, None),
        P("space", "inst", None),
        P(None, "space", "inst"),
        P("space", "inst"),
    )
    out_specs = (P(None, "space", "inst", None), P(("inst", "space")))
    return jax.shard_map(
        per_device, mesh=mesh, in_specs=in_specs, out_specs=out_specs, check_vma=False
    )
```

```python
import functools

import jax
import jax.numpy as jnp
from jax import lax
from jax.experimental import pallas as pl
from jax.experimental.pallas import tpu as pltpu
from jax.sharding import PartitionSpec as P

F32 = jnp.float32
MESH = pl.DeviceIdType.MESH
A = 1.0 / 6.5
ROWS = 4
STARTS = (0, 12, 4, 8)
CHUNKS = tuple((zh, x0) for zh in range(2) for x0 in STARTS)
LAG = 3
YZ = 16
REACH = (1, 2, 4, 8)


def iota(shape, axis):
    return lax.broadcasted_iota(jnp.int32, shape, axis)


def roll(value, shift, axis):
    return pltpu.roll(value, shift % value.shape[axis], axis)


def kernel(
    adj, flux, stiff, normals, dmap, lam_ref, dg_ref,
    av, fv, kv, nv, dv, q, rc, g, xr, ps, pr, w, vg, m1, dsum, ra, rb,
    load_sem, small_sem, c_send, c_recv, x_send, x_recv, h_send, h_recv,
    p_send, p_recv, n_send, n_recv, a_send, a_recv, b_send, b_recv, ring_sem,
):
    inst = lax.axis_index("inst")
    s = lax.axis_index("space")
    h = inst // 2
    c = lax.rem(inst, 2)
    xlo = lax.rem(s, 2)
    yz = s // 2
    partner = (2 * h + 1 - c, s)
    opposite = (2 * (1 - h) + c, s)
    up_dev = (inst, lax.rem(s + 1, 32))
    down_dev = (inst, lax.rem(s + 31, 32))
    has_up = s < 31
    has_down = s > 0
    sends_halo = c == h
    sub = iota((8, 128), 0)
    lane = iota((8, 128), 1)
    zero = jnp.zeros((8, 128), F32)

    loads = []
    for t, (zh, x0) in enumerate(CHUNKS):
        rows, zs = pl.ds(x0, ROWS), pl.ds(zh * 128, 128)
        pair = [
            pltpu.make_async_copy(
                adj.at[:, :, rows, :, zs], av.at[zh, :, :, rows], load_sem.at[t, 0]
            ),
            pltpu.make_async_copy(
                flux.at[:, :, :, rows, :, zs], fv.at[zh, :, :, :, rows], load_sem.at[t, 1]
            ),
        ]
        for copy in pair:
            copy.start()
        loads.append(pair)
    small = [
        pltpu.make_async_copy(stiff, kv, small_sem.at[0]),
        pltpu.make_async_copy(normals, nv, small_sem.at[1]),
        pltpu.make_async_copy(dmap, dv, small_sem.at[2]),
    ]
    for copy in small:
        copy.start()

    def clear(x, _):
        for zh in range(2):
            xr[zh, x, 3] = zero
        return 0

    lax.fori_loop(0, 16, clear, 0)
    for zh in range(2):
        for row in (0, 1, 2, 19, 20, 21):
            for tile in range(6):
                w[zh, row, tile] = zero

    barrier = pltpu.get_barrier_semaphore()

    for device in (partner, opposite, up_dev, down_dev):
        pl.semaphore_signal(barrier, inc=1, device_id=device, device_id_type=MESH)
    mine = inst * 2 + xlo

    def x_peer(j):
        other = lax.rem(mine + j, 8)
        return (other // 2, yz * 2 + lax.rem(other, 2))

    def ring_signal(r):
        for step in (REACH[r], 32 - REACH[r]):
            pl.semaphore_signal(
                ring_sem.at[r], inc=1, device_id=(inst, lax.rem(s + step, 32)),
                device_id_type=MESH,
            )

    def ring_wait(r):
        pl.semaphore_wait(ring_sem.at[r], 2)

    def remote(src, dst, send, recv, device):
        return pltpu.make_async_remote_copy(
            src_ref=src, dst_ref=dst, send_sem=send, recv_sem=recv,
            device_id=device, device_id_type=MESH,
        )

    def pack_up(w0, w1, w2):
        return jnp.where(sub < 2, w0, jnp.where(sub < 4, roll(w2, 2, 0), roll(w1, 4, 0)))

    def pack_low(w0, w1, w2):
        return jnp.where(sub >= 6, w0, jnp.where(sub >= 4, roll(w2, 6, 0), roll(w1, 4, 0)))

    def slot(block, core):
        rb = block + h - 2 * block * h
        rk = core + c - 2 * core * c
        return rk * 3 * rb + (1 - rk) * (11 - 4 * rb)

    def core_copy(t):
        zh, x0 = CHUNKS[t]
        rows = pl.ds(x0, ROWS)
        return remote(
            q.at[zh, rows, pl.ds(0, 7)], rc.at[zh, rows], c_send.at[t], c_recv.at[t], partner
        )

    def cross_copy(t):
        zh, x0 = CHUNKS[t]
        rows = pl.ds(x0, ROWS)
        main = pl.ds(0, 3)
        return remote(
            g.at[zh, rows, main], xr.at[zh, rows, main], x_send.at[t], x_recv.at[t], opposite
        )

    def halo_copy(t):
        zh, x0 = CHUNKS[t]
        rows = pl.ds(x0, ROWS)
        last = pl.ds(3, 1)
        return remote(
            g.at[zh, rows, last], xr.at[zh, rows, last], h_send.at[t], h_recv.at[t], opposite
        )

    def pair_copy(t):
        zh, x0 = CHUNKS[t]
        rows = pl.ds(x0, ROWS)
        return remote(ps.at[zh, rows], pr.at[zh, rows], p_send.at[t], p_recv.at[t], partner)

    def partial(t):
        zh, x0 = CHUNKS[t]
        for copy in loads[t]:
            copy.wait()

        def row(r, _):
            x = x0 + r
            tiles = {}
            for block in range(2):
                ys = pl.ds(16 * block, 16)
                acc = [None] * 3
                for k in range(2):
                    for v in range(5):
                        a = av[zh, k, v, x, ys, :].astype(F32)
                        for d in range(3):
                            term = a * fv[zh, k, v, d, x, ys, :].astype(F32)
                            acc[d] = term if acc[d] is None else acc[d] + term
                for core in range(2):
                    base = slot(block, core)
                    for d in range(3):
                        tile = acc[d][8 * core : 8 * core + 8]
                        tiles[block, core, d] = tile
                        q[zh, x, base + d] = tile
            q[zh, x, 6 + 4 * c] = pack_up(*[tiles[1, 0, d] for d in range(3)])
            q[zh, x, 10 - 4 * c] = pack_low(*[tiles[0, 1, d] for d in range(3)])
            return 0

        lax.fori_loop(0, ROWS, row, 0)
        if t == 0:
            pl.semaphore_wait(barrier, 4)
            ring_signal(0)
        core_copy(t).start()

    def cross(t):
        zh, x0 = CHUNKS[t]
        core_copy(t).wait_recv()

        def row(r, _):
            x = x0 + r
            for d in range(4):
                g[zh, x, d] = q[zh, x, 7 + d] + rc[zh, x, 3 + d]
            return 0

        lax.fori_loop(0, ROWS, row, 0)
        cross_copy(t).start()

        @pl.when(sends_halo)
        def _():
            halo_copy(t).start()

    def finish(t):
        zh, x0 = CHUNKS[t]
        cross_copy(t).wait_recv()

        def row(r, _):
            x = x0 + r
            own = [q[zh, x, 11 + d] + rc[zh, x, d] + xr[zh, x, d] for d in range(3)]
            w[zh, x + 3, 0] = own[0]
            w[zh, x + 3, 2] = own[1]
            w[zh, x + 3, 3] = own[2]
            ps[zh, x] = jnp.where(c == 0, pack_low(*own), pack_up(*own))
            return 0

        lax.fori_loop(0, ROWS, row, 0)
        pair_copy(t).start()

    def halo(t):
        zh, x0 = CHUNKS[t]
        pair_copy(t).wait_recv()

        @pl.when(jnp.logical_not(sends_halo))
        def _():
            halo_copy(t).wait_recv()

        def row(r, _):
            x = x0 + r
            far = jnp.where(sends_halo, zero, g[zh, x, 3] + xr[zh, x, 3])
            near = pr[zh, x]
            top = jnp.where(c == 0, near, far)
            low = jnp.where(c == 0, far, near)
            w[zh, x + 3, 1] = jnp.where(sub < 2, top, jnp.where(sub >= 6, low, 0.0))
            w[zh, x + 3, 4] = jnp.where(
                sub < 3, roll(top, 4, 0), jnp.where(sub >= 5, roll(low, 4, 0), 0.0)
            )
            w[zh, x + 3, 5] = jnp.where(
                sub < 2, roll(top, 6, 0), jnp.where(sub >= 6, roll(low, 2, 0), 0.0)
            )
            return 0

        lax.fori_loop(0, ROWS, row, 0)

    def side_copies(zh, side):
        out = []
        for j, width in enumerate((6, 5, 1)):
            src = 18 - j if side == 0 else 3 + j
            dst = 2 - j if side == 0 else 19 + j
            tiles = pl.ds(0, width)
            out.append(
                remote(
                    w.at[zh, src, tiles], w.at[zh, dst, tiles],
                    n_send.at[zh, side, j], n_recv.at[zh, side, j],
                    up_dev if side == 0 else down_dev,
                )
            )
        return out

    def side_send(zh):
        for side, there in ((0, has_up), (1, has_down)):
            @pl.when(there)
            def _(side=side):
                for copy in side_copies(zh, side):
                    copy.start()

    def side_wait(zh):
        for side, there in ((0, has_down), (1, has_up)):
            @pl.when(there)
            def _(side=side):
                for copy in side_copies(zh, side):
                    copy.wait_recv()

    up_ok = (inst < 3).astype(F32)
    low_ok = (inst > 0).astype(F32)
    ring_mask = jnp.where(sub < 4, up_ok, low_ok)
    x_low_ok = has_down.astype(F32)
    x_up_ok = has_up.astype(F32)

    def x_mask(row):
        return jnp.where(row < 3, x_low_ok, jnp.where(row > 18, x_up_ok, 1.0))

    def y_before(own, ring):
        a, b = roll(own, 1, 0), roll(ring, 1, 0)
        return jnp.where(sub == 0, b, a), jnp.where(sub == 0, a, b)

    def y_after(own, ring):
        a, b = roll(own, 7, 0), roll(ring, 7, 0)
        return jnp.where(sub == 7, b, a), jnp.where(sub == 7, a, b)

    def z_before(parts):
        turned = [roll(p, 1, 1) for p in parts]
        return [
            jnp.where(lane == 0, turned[z - 1] if z else 0.0, turned[z]) for z in range(len(parts))
        ]

    def z_after(parts):
        turned = [roll(p, 127, 1) for p in parts]
        last = len(parts) - 1
        return [
            jnp.where(lane == 127, turned[z + 1] if z < last else 0.0, turned[z])
            for z in range(len(parts))
        ]

    own_at = (0, 2, 3)
    ring_at = (1, 4, 5)

    def gradient(halves):
        zs = range(halves)

        def row(x, _):
            xm = x_mask(x)
            rm = ring_mask * xm
            for tile, at in ((0, own_at), (1, ring_at)):
                m = xm if tile == 0 else rm
                for z in zs:
                    mid = w[z, x, at[0]]
                    diff = w[z, x - 1, at[0]] - w[z, x + 1, at[0]]
                    vg[z, x, 0, tile] = (mid + 0.5 * diff) * m
                parts = [w[z, x, at[2]] for z in zs]
                before, after = z_before(parts), z_after(parts)
                for z in zs:
                    vg[z, x, 2, tile] = (parts[z] + 0.5 * (before[z] - after[z])) * m
            for z in zs:
                own, ring = w[z, x, own_at[1]], w[z, x, ring_at[1]]
                before, after = y_before(own, ring), y_after(own, ring)
                vg[z, x, 1, 0] = (own + 0.5 * (before[0] - after[0])) * xm
                vg[z, x, 1, 1] = (ring + 0.5 * (before[1] - after[1])) * rm
            return 0

        lax.fori_loop(1, 21, row, 0)

    def around(ref, x, d, zs, tiles):
        own = [ref[z, x, d, 0] for z in zs]
        ring = [ref[z, x, d, 1] for z in zs]
        total = {}
        for z in zs:
            before, after = y_before(own[z], ring[z]), y_after(own[z], ring[z])
            for tile in tiles:
                total[z, tile] = (
                    before[tile] + after[tile] + ref[z, x - 1, d, tile] + ref[z, x + 1, d, tile]
                )
        for tile in tiles:
            parts = own if tile == 0 else ring
            before, after = z_before(parts), z_after(parts)
            for z in zs:
                total[z, tile] = total[z, tile] + before[z] + after[z]
        return total

    def sweep(halves):
        zs = range(halves)

        def row(x, _):
            xm = x_mask(x) * A
            rm = ring_mask * xm
            for d in range(3):
                total = around(vg, x, d, zs, (0, 1))
                for z in zs:
                    m1[z, x, d, 0] = (vg[z, x, d, 0] + A * total[z, 0]) * xm
                    m1[z, x, d, 1] = (vg[z, x, d, 1] + A * total[z, 1]) * rm
            return 0

        lax.fori_loop(2, 20, row, 0)

    def last_sweep(x, halves):
        zs = range(halves)
        out = [[None] * 3 for _ in zs]
        for z in zs:
            out[z] = [None] * 3
        scale = [0.125 / (6.5 * kv[x, :, 128 * z : 128 * z + 128]) for z in zs]
        for d in range(3):
            total = around(m1, x + 3, d, zs, (0,))
            for z in zs:
                out[z][d] = (vg[z, x + 3, d, 0] + total[z, 0]) * scale[z]
        return out

    def yz_copy(j):
        target = (inst, lax.rem(yz + j, YZ) * 2 + xlo)
        return remote(dsum.at[0], ra.at[j], a_send.at[j], a_recv.at[j], target)

    def x_copy(j):
        return remote(dsum.at[1], rb.at[j], b_send.at[j], b_recv.at[j], x_peer(j))

    def design_start():
        gradient(1)
        sweep(1)
        small[0].wait()

        def row(x, wall):
            lam = last_sweep(x, 1)[0]
            return tuple(
                jnp.where(lane == x, jnp.broadcast_to(lam[d][:, 0:1], (8, 128)), wall[d])
                for d in range(3)
            )

        wall = lax.fori_loop(0, 16, row, (zero, zero, zero))
        small[1].wait()
        small[2].wait()
        surface = sum(nv[d] * wall[d][:, :16] for d in range(3))
        ids = dv[...]
        values = jnp.concatenate([surface[y : y + 1, :] for y in range(8)], axis=1)
        flat = jnp.concatenate([ids[y : y + 1, :] for y in range(8)], axis=1)
        high, low = flat // 128, lax.rem(flat, 128)
        left = jnp.where(
            jnp.broadcast_to(high, (8, 128)) == sub, jnp.broadcast_to(values, (8, 128)), 0.0
        )
        right = (jnp.broadcast_to(low, (128, 128)) == iota((128, 128), 0)).astype(F32)
        dsum[0] = lax.dot_general(
            left, right, (((1,), (1,)), ((), ())),
            precision=lax.Precision.HIGHEST, preferred_element_type=F32,
        )

        def send(j, _):
            yz_copy(j).start()
            return 0

        lax.fori_loop(1, YZ, send, 0)

    def design_middle():
        def take(j, total):
            yz_copy(j).wait_recv()
            return total + ra[j]

        dsum[1] = lax.fori_loop(1, YZ, take, dsum[0])
        for j in range(1, 8):
            x_copy(j).start()

    def design_end():
        total = dsum[1]
        for j in range(1, 8):
            x_copy(j).wait_recv()
            total = total + rb[j]
        device = inst * 32 + s
        picked = jnp.where(sub == device // 16, total, 0.0)
        line = jnp.broadcast_to(jnp.sum(picked, axis=0, keepdims=True), (8, 128))
        turned = pltpu.roll(line, lax.rem(128 - lax.rem(device, 16) * 8, 128), 1)
        dg_ref[...] = turned[0:1, :8]

    count = len(CHUNKS)
    for t in range(count + LAG + 3):
        if t < count:
            partial(t)
        if 0 <= t - 1 < count:
            cross(t - 1)
        if 0 <= t - 1 - LAG < count:
            finish(t - 1 - LAG)
        done = t - 2 - LAG
        if 0 <= done < count:
            halo(done)
            if done < 4:
                ring_wait(done)
            if done < 3:
                ring_signal(done + 1)
            if done % 4 == 1:
                side_send(done // 4)
            if done == 3:
                side_wait(0)
                design_start()
            if done == 6:
                design_middle()
    side_wait(1)
    gradient(2)
    sweep(2)

    def emit(x, _):
        lam = last_sweep(x, 2)
        for z in range(2):
            for d in range(3):
                lam_ref[d, x, :, 128 * z : 128 * z + 128] = lam[z][d]
        return 0

    lax.fori_loop(0, 16, emit, 0)
    design_end()

    for t in range(count):
        core_copy(t).wait_send()
        cross_copy(t).wait_send()
        pair_copy(t).wait_send()

    @pl.when(sends_halo)
    def _():
        for t in range(count):
            halo_copy(t).wait_send()

    for zh in range(2):
        for side, there in ((0, has_up), (1, has_down)):
            @pl.when(there)
            def _(zh=zh, side=side):
                for copy in side_copies(zh, side):
                    copy.wait_send()

    def drain(j, _):
        yz_copy(j).wait_send()
        return 0

    lax.fori_loop(1, YZ, drain, 0)
    for j in range(1, 8):
        x_copy(j).wait_send()


def per_device(adjoint, flux_terms, stiffness, normals, design_map):
    hbm = pl.BlockSpec(memory_space=pl.ANY)
    dma = pltpu.SemaphoreType.DMA
    count = len(CHUNKS)

    def tiles(*lead):
        return pltpu.VMEM(lead + (8, 128), F32)

    lam, grad = pl.pallas_call(
        kernel,
        out_shape=(
            jax.ShapeDtypeStruct((3, 16, 8, 256), F32),
            jax.ShapeDtypeStruct((1, 8), F32),
        ),
        in_specs=[hbm] * 5,
        out_specs=(
            pl.BlockSpec(memory_space=pltpu.VMEM),
            pl.BlockSpec(memory_space=pltpu.VMEM),
        ),
        scratch_shapes=[
            pltpu.VMEM((2, 2, 5, 16, 32, 128), jnp.bfloat16),
            pltpu.VMEM((2, 2, 5, 3, 16, 32, 128), jnp.bfloat16),
            pltpu.VMEM((16, 8, 256), F32),
            pltpu.VMEM((3, 8, 16), F32),
            pltpu.VMEM((8, 16), jnp.int32),
            tiles(2, 16, 14),
            tiles(2, 16, 7),
            tiles(2, 16, 4),
            tiles(2, 16, 4),
            tiles(2, 16),
            tiles(2, 16),
            tiles(2, 22, 6),
            tiles(2, 22, 3, 2),
            tiles(2, 22, 3, 2),
            tiles(2),
            tiles(YZ),
            tiles(8),
            dma((count, 2)),
            dma((3,)),
            dma((count,)), dma((count,)), dma((count,)), dma((count,)),
            dma((count,)), dma((count,)), dma((count,)), dma((count,)),
            dma((2, 2, 3)), dma((2, 2, 3)),
            dma((YZ,)), dma((YZ,)), dma((8,)), dma((8,)),
            pltpu.SemaphoreType.REGULAR((4,)),
        ],
        compiler_params=pltpu.CompilerParams(
            collective_id=0, has_side_effects=True, vmem_limit_bytes=60 * 1024 * 1024
        ),
    )(adjoint, flux_terms, stiffness, normals.transpose(0, 2, 1), design_map.T)
    return lam, grad.reshape(8)


def solution(mesh):
    in_specs = (
        P("inst", None, "space", None, None),
        P("inst", None, None, "space", None, None),
        P("space", "inst", None),
        P(None, "space", "inst"),
        P("space", "inst"),
    )
    out_specs = (P(None, "space", "inst", None), P(("inst", "space")))
    return jax.shard_map(
        per_device, mesh=mesh, in_specs=in_specs, out_specs=out_specs, check_vma=False
    )
```

```python
import functools

import jax
import jax.numpy as jnp
from jax import lax
from jax.experimental import pallas as pl
from jax.experimental.pallas import tpu as pltpu
from jax.sharding import PartitionSpec as P

F32 = jnp.float32
MESH = pl.DeviceIdType.MESH
A = 1.0 / 6.5
ROWS = 4
STARTS = (0, 12, 4, 8)
CHUNKS = tuple((zh, x0) for zh in range(2) for x0 in STARTS)
LAG = 3
YZ = 16
REACH = (1, 2, 4, 8)


def iota(shape, axis):
    return lax.broadcasted_iota(jnp.int32, shape, axis)


def roll(value, shift, axis):
    return pltpu.roll(value, shift % value.shape[axis], axis)


def kernel(
    adj, flux, stiff, normals, dmap, lam_ref, dg_ref,
    av, fv, kv, nv, dv, q, rc, g, xr, ps, pr, w, vg, m1, dsum, ra, rb,
    load_sem, small_sem, c_send, c_recv, x_send, x_recv, h_send, h_recv,
    p_send, p_recv, n_send, n_recv, a_send, a_recv, b_send, b_recv, ring_sem,
):
    inst = lax.axis_index("inst")
    s = lax.axis_index("space")
    h = inst // 2
    c = lax.rem(inst, 2)
    xlo = lax.rem(s, 2)
    yz = s // 2
    partner = (2 * h + 1 - c, s)
    opposite = (2 * (1 - h) + c, s)
    up_dev = (inst, lax.rem(s + 1, 32))
    down_dev = (inst, lax.rem(s + 31, 32))
    has_up = s < 31
    has_down = s > 0
    sends_halo = c == h
    sub = iota((8, 128), 0)
    lane = iota((8, 128), 1)
    zero = jnp.zeros((8, 128), F32)

    loads = []
    for t, (zh, x0) in enumerate(CHUNKS):
        rows, zs = pl.ds(x0, ROWS), pl.ds(zh * 128, 128)
        pair = [
            pltpu.make_async_copy(
                adj.at[:, :, rows, :, zs], av.at[zh, :, :, rows], load_sem.at[t, 0]
            ),
            pltpu.make_async_copy(
                flux.at[:, :, :, rows, :, zs], fv.at[zh, :, :, :, rows], load_sem.at[t, 1]
            ),
        ]
        for copy in pair:
            copy.start()
        loads.append(pair)
    small = [
        pltpu.make_async_copy(stiff, kv, small_sem.at[0]),
        pltpu.make_async_copy(normals, nv, small_sem.at[1]),
        pltpu.make_async_copy(dmap, dv, small_sem.at[2]),
    ]
    for copy in small:
        copy.start()

    def clear(x, _):
        for zh in range(2):
            xr[zh, x, 3] = zero
        return 0

    lax.fori_loop(0, 16, clear, 0)
    for zh in range(2):
        for row in (0, 1, 2, 19, 20, 21):
            for tile in range(6):
                w[zh, row, tile] = zero

    barrier = pltpu.get_barrier_semaphore()

    for device in (partner, opposite, up_dev, down_dev):
        pl.semaphore_signal(barrier, inc=1, device_id=device, device_id_type=MESH)
    mine = inst * 2 + xlo

    def x_peer(j):
        other = lax.rem(mine + j, 8)
        return (other // 2, yz * 2 + lax.rem(other, 2))

    def ring_signal(r):
        for step in (REACH[r], 32 - REACH[r]):
            pl.semaphore_signal(
                ring_sem.at[r], inc=1, device_id=(inst, lax.rem(s + step, 32)),
                device_id_type=MESH,
            )

    def ring_wait(r):
        pl.semaphore_wait(ring_sem.at[r], 2)

    def remote(src, dst, send, recv, device):
        return pltpu.make_async_remote_copy(
            src_ref=src, dst_ref=dst, send_sem=send, recv_sem=recv,
            device_id=device, device_id_type=MESH,
        )

    def pack_up(w0, w1, w2):
        return jnp.where(sub < 2, w0, jnp.where(sub < 4, roll(w2, 2, 0), roll(w1, 4, 0)))

    def pack_low(w0, w1, w2):
        return jnp.where(sub >= 6, w0, jnp.where(sub >= 4, roll(w2, 6, 0), roll(w1, 4, 0)))

    def slot(block, core):
        rb = block + h - 2 * block * h
        rk = core + c - 2 * core * c
        return rk * 3 * rb + (1 - rk) * (11 - 4 * rb)

    def core_copy(t):
        zh, x0 = CHUNKS[t]
        rows = pl.ds(x0, ROWS)
        return remote(
            q.at[zh, rows, pl.ds(0, 7)], rc.at[zh, rows], c_send.at[t], c_recv.at[t], partner
        )

    def cross_copy(t):
        zh, x0 = CHUNKS[t]
        rows = pl.ds(x0, ROWS)
        main = pl.ds(0, 3)
        return remote(
            g.at[zh, rows, main], xr.at[zh, rows, main], x_send.at[t], x_recv.at[t], opposite
        )

    def halo_copy(t):
        zh, x0 = CHUNKS[t]
        rows = pl.ds(x0, ROWS)
        last = pl.ds(3, 1)
        return remote(
            g.at[zh, rows, last], xr.at[zh, rows, last], h_send.at[t], h_recv.at[t], opposite
        )

    def pair_copy(t):
        zh, x0 = CHUNKS[t]
        rows = pl.ds(x0, ROWS)
        return remote(ps.at[zh, rows], pr.at[zh, rows], p_send.at[t], p_recv.at[t], partner)

    def partial(t):
        zh, x0 = CHUNKS[t]
        for copy in loads[t]:
            copy.wait()

        def row(r, _):
            x = x0 + r
            tiles = {}
            for block in range(2):
                ys = pl.ds(16 * block, 16)
                acc = [None] * 3
                for k in range(2):
                    for v in range(5):
                        a = av[zh, k, v, x, ys, :].astype(F32)
                        for d in range(3):
                            term = a * fv[zh, k, v, d, x, ys, :].astype(F32)
                            acc[d] = term if acc[d] is None else acc[d] + term
                for core in range(2):
                    base = slot(block, core)
                    for d in range(3):
                        tile = acc[d][8 * core : 8 * core + 8]
                        tiles[block, core, d] = tile
                        q[zh, x, base + d] = tile
            q[zh, x, 6 + 4 * c] = pack_up(*[tiles[1, 0, d] for d in range(3)])
            q[zh, x, 10 - 4 * c] = pack_low(*[tiles[0, 1, d] for d in range(3)])
            return 0

        lax.fori_loop(0, ROWS, row, 0)
        if t == 0:
            pl.semaphore_wait(barrier, 4)
            ring_signal(0)
        core_copy(t).start()

    def cross(t):
        zh, x0 = CHUNKS[t]
        core_copy(t).wait_recv()

        def row(r, _):
            x = x0 + r
            for d in range(4):
                g[zh, x, d] = q[zh, x, 7 + d] + rc[zh, x, 3 + d]
            return 0

        lax.fori_loop(0, ROWS, row, 0)
        cross_copy(t).start()

        @pl.when(sends_halo)
        def _():
            halo_copy(t).start()

    def finish(t):
        zh, x0 = CHUNKS[t]
        cross_copy(t).wait_recv()

        def row(r, _):
            x = x0 + r
            own = [q[zh, x, 11 + d] + rc[zh, x, d] + xr[zh, x, d] for d in range(3)]
            w[zh, x + 3, 0] = own[0]
            w[zh, x + 3, 2] = own[1]
            w[zh, x + 3, 3] = own[2]
            ps[zh, x] = jnp.where(c == 0, pack_low(*own), pack_up(*own))
            return 0

        lax.fori_loop(0, ROWS, row, 0)
        pair_copy(t).start()

    def halo(t):
        zh, x0 = CHUNKS[t]
        pair_copy(t).wait_recv()

        @pl.when(jnp.logical_not(sends_halo))
        def _():
            halo_copy(t).wait_recv()

        def row(r, _):
            x = x0 + r
            far = jnp.where(sends_halo, zero, g[zh, x, 3] + xr[zh, x, 3])
            near = pr[zh, x]
            top = jnp.where(c == 0, near, far)
            low = jnp.where(c == 0, far, near)
            w[zh, x + 3, 1] = jnp.where(sub < 2, top, jnp.where(sub >= 6, low, 0.0))
            w[zh, x + 3, 4] = jnp.where(
                sub < 3, roll(top, 4, 0), jnp.where(sub >= 5, roll(low, 4, 0), 0.0)
            )
            w[zh, x + 3, 5] = jnp.where(
                sub < 2, roll(top, 6, 0), jnp.where(sub >= 6, roll(low, 2, 0), 0.0)
            )
            return 0

        lax.fori_loop(0, ROWS, row, 0)

    def side_copies(zh, side):
        out = []
        for j, width in enumerate((6, 5, 1)):
            src = 18 - j if side == 0 else 3 + j
            dst = 2 - j if side == 0 else 19 + j
            tiles = pl.ds(0, width)
            out.append(
                remote(
                    w.at[zh, src, tiles], w.at[zh, dst, tiles],
                    n_send.at[zh, side, j], n_recv.at[zh, side, j],
                    up_dev if side == 0 else down_dev,
                )
            )
        return out

    def side_send(zh):
        for side, there in ((0, has_up), (1, has_down)):
            @pl.when(there)
            def _(side=side):
                for copy in side_copies(zh, side):
                    copy.start()

    def side_wait(zh):
        for side, there in ((0, has_down), (1, has_up)):
            @pl.when(there)
            def _(side=side):
                for copy in side_copies(zh, side):
                    copy.wait_recv()

    up_ok = (inst < 3).astype(F32)
    low_ok = (inst > 0).astype(F32)
    ring_mask = jnp.where(sub < 4, up_ok, low_ok)
    x_low_ok = has_down.astype(F32)
    x_up_ok = has_up.astype(F32)

    def x_mask(row):
        return jnp.where(row < 3, x_low_ok, jnp.where(row > 18, x_up_ok, 1.0))

    def y_before(own, ring):
        a, b = roll(own, 1, 0), roll(ring, 1, 0)
        return jnp.where(sub == 0, b, a), jnp.where(sub == 0, a, b)

    def y_after(own, ring):
        a, b = roll(own, 7, 0), roll(ring, 7, 0)
        return jnp.where(sub == 7, b, a), jnp.where(sub == 7, a, b)

    def z_before(parts):
        turned = [roll(p, 1, 1) for p in parts]
        return [
            jnp.where(lane == 0, turned[z - 1] if z else 0.0, turned[z]) for z in range(len(parts))
        ]

    def z_after(parts):
        turned = [roll(p, 127, 1) for p in parts]
        last = len(parts) - 1
        return [
            jnp.where(lane == 127, turned[z + 1] if z < last else 0.0, turned[z])
            for z in range(len(parts))
        ]

    own_at = (0, 2, 3)
    ring_at = (1, 4, 5)

    def gradient(halves):
        zs = range(halves)
        fresh = range(halves - 1, halves)

        def row(x, _):
            xm = x_mask(x)
            rm = ring_mask * xm
            for tile, at in ((0, own_at), (1, ring_at)):
                m = xm if tile == 0 else rm
                for z in fresh:
                    mid = w[z, x, at[0]]
                    diff = w[z, x - 1, at[0]] - w[z, x + 1, at[0]]
                    vg[z, x, 0, tile] = (mid + 0.5 * diff) * m
                parts = [w[z, x, at[2]] for z in zs]
                before, after = z_before(parts), z_after(parts)
                for z in zs:
                    vg[z, x, 2, tile] = (parts[z] + 0.5 * (before[z] - after[z])) * m
            for z in fresh:
                own, ring = w[z, x, own_at[1]], w[z, x, ring_at[1]]
                before, after = y_before(own, ring), y_after(own, ring)
                vg[z, x, 1, 0] = (own + 0.5 * (before[0] - after[0])) * xm
                vg[z, x, 1, 1] = (ring + 0.5 * (before[1] - after[1])) * rm
            return 0

        lax.fori_loop(1, 21, row, 0)

    def around(ref, x, d, zs, tiles):
        own = [ref[z, x, d, 0] for z in zs]
        ring = [ref[z, x, d, 1] for z in zs]
        total = {}
        for z in zs:
            before, after = y_before(own[z], ring[z]), y_after(own[z], ring[z])
            for tile in tiles:
                total[z, tile] = (
                    before[tile] + after[tile] + ref[z, x - 1, d, tile] + ref[z, x + 1, d, tile]
                )
        for tile in tiles:
            parts = own if tile == 0 else ring
            before, after = z_before(parts), z_after(parts)
            for z in zs:
                total[z, tile] = total[z, tile] + before[z] + after[z]
        return total

    def sweep(halves):
        zs = range(halves)

        def row(x, _):
            xm = x_mask(x) * A
            rm = ring_mask * xm
            for d in range(3):
                total = around(vg, x, d, zs, (0, 1))
                for z in zs:
                    m1[z, x, d, 0] = (vg[z, x, d, 0] + A * total[z, 0]) * xm
                    m1[z, x, d, 1] = (vg[z, x, d, 1] + A * total[z, 1]) * rm
            return 0

        lax.fori_loop(2, 20, row, 0)

    def last_sweep(x, halves):
        zs = range(halves)
        out = [[None] * 3 for _ in zs]
        for z in zs:
            out[z] = [None] * 3
        scale = [0.125 / (6.5 * kv[x, :, 128 * z : 128 * z + 128]) for z in zs]
        for d in range(3):
            total = around(m1, x + 3, d, zs, (0,))
            for z in zs:
                out[z][d] = (vg[z, x + 3, d, 0] + total[z, 0]) * scale[z]
        return out

    def yz_copy(j):
        target = (inst, lax.rem(yz + j, YZ) * 2 + xlo)
        return remote(dsum.at[0], ra.at[j], a_send.at[j], a_recv.at[j], target)

    def x_copy(j):
        return remote(dsum.at[1], rb.at[j], b_send.at[j], b_recv.at[j], x_peer(j))

    def design_start():
        gradient(1)
        sweep(1)
        small[0].wait()

        def row(x, wall):
            lam = last_sweep(x, 1)[0]
            return tuple(
                jnp.where(lane == x, jnp.broadcast_to(lam[d][:, 0:1], (8, 128)), wall[d])
                for d in range(3)
            )

        wall = lax.fori_loop(0, 16, row, (zero, zero, zero))
        small[1].wait()
        small[2].wait()
        surface = sum(nv[d] * wall[d][:, :16] for d in range(3))
        ids = dv[...]
        values = jnp.concatenate([surface[y : y + 1, :] for y in range(8)], axis=1)
        flat = jnp.concatenate([ids[y : y + 1, :] for y in range(8)], axis=1)
        high, low = flat // 128, lax.rem(flat, 128)
        left = jnp.where(
            jnp.broadcast_to(high, (8, 128)) == sub, jnp.broadcast_to(values, (8, 128)), 0.0
        )
        right = (jnp.broadcast_to(low, (128, 128)) == iota((128, 128), 0)).astype(F32)
        dsum[0] = lax.dot_general(
            left, right, (((1,), (1,)), ((), ())),
            precision=lax.Precision.HIGHEST, preferred_element_type=F32,
        )

        def send(j, _):
            yz_copy(j).start()
            return 0

        lax.fori_loop(1, YZ, send, 0)

    def design_middle():
        def take(j, total):
            yz_copy(j).wait_recv()
            return total + ra[j]

        dsum[1] = lax.fori_loop(1, YZ, take, dsum[0])
        for j in range(1, 8):
            x_copy(j).start()

    def design_end():
        total = dsum[1]
        for j in range(1, 8):
            x_copy(j).wait_recv()
            total = total + rb[j]
        device = inst * 32 + s
        picked = jnp.where(sub == device // 16, total, 0.0)
        line = jnp.broadcast_to(jnp.sum(picked, axis=0, keepdims=True), (8, 128))
        turned = pltpu.roll(line, lax.rem(128 - lax.rem(device, 16) * 8, 128), 1)
        dg_ref[...] = turned[0:1, :8]

    count = len(CHUNKS)
    for t in range(count + LAG + 3):
        if t < count:
            partial(t)
        if 0 <= t - 1 < count:
            cross(t - 1)
        if 0 <= t - 1 - LAG < count:
            finish(t - 1 - LAG)
        done = t - 2 - LAG
        if 0 <= done < count:
            halo(done)
            if done < 4:
                ring_wait(done)
            if done < 3:
                ring_signal(done + 1)
            if done % 4 == 1:
                side_send(done // 4)
            if done == 5:
                side_wait(0)
                design_start()
    side_wait(1)
    gradient(2)
    design_middle()
    sweep(2)

    def emit(x, _):
        lam = last_sweep(x, 2)
        for z in range(2):
            for d in range(3):
                lam_ref[d, x, :, 128 * z : 128 * z + 128] = lam[z][d]
        return 0

    lax.fori_loop(0, 16, emit, 0)
    design_end()

    for t in range(count):
        core_copy(t).wait_send()
        cross_copy(t).wait_send()
        pair_copy(t).wait_send()

    @pl.when(sends_halo)
    def _():
        for t in range(count):
            halo_copy(t).wait_send()

    for zh in range(2):
        for side, there in ((0, has_up), (1, has_down)):
            @pl.when(there)
            def _(zh=zh, side=side):
                for copy in side_copies(zh, side):
                    copy.wait_send()

    def drain(j, _):
        yz_copy(j).wait_send()
        return 0

    lax.fori_loop(1, YZ, drain, 0)
    for j in range(1, 8):
        x_copy(j).wait_send()


def per_device(adjoint, flux_terms, stiffness, normals, design_map):
    hbm = pl.BlockSpec(memory_space=pl.ANY)
    dma = pltpu.SemaphoreType.DMA
    count = len(CHUNKS)

    def tiles(*lead):
        return pltpu.VMEM(lead + (8, 128), F32)

    lam, grad = pl.pallas_call(
        kernel,
        out_shape=(
            jax.ShapeDtypeStruct((3, 16, 8, 256), F32),
            jax.ShapeDtypeStruct((1, 8), F32),
        ),
        in_specs=[hbm] * 5,
        out_specs=(
            pl.BlockSpec(memory_space=pltpu.VMEM),
            pl.BlockSpec(memory_space=pltpu.VMEM),
        ),
        scratch_shapes=[
            pltpu.VMEM((2, 2, 5, 16, 32, 128), jnp.bfloat16),
            pltpu.VMEM((2, 2, 5, 3, 16, 32, 128), jnp.bfloat16),
            pltpu.VMEM((16, 8, 256), F32),
            pltpu.VMEM((3, 8, 16), F32),
            pltpu.VMEM((8, 16), jnp.int32),
            tiles(2, 16, 14),
            tiles(2, 16, 7),
            tiles(2, 16, 4),
            tiles(2, 16, 4),
            tiles(2, 16),
            tiles(2, 16),
            tiles(2, 22, 6),
            tiles(2, 22, 3, 2),
            tiles(2, 22, 3, 2),
            tiles(2),
            tiles(YZ),
            tiles(8),
            dma((count, 2)),
            dma((3,)),
            dma((count,)), dma((count,)), dma((count,)), dma((count,)),
            dma((count,)), dma((count,)), dma((count,)), dma((count,)),
            dma((2, 2, 3)), dma((2, 2, 3)),
            dma((YZ,)), dma((YZ,)), dma((8,)), dma((8,)),
            pltpu.SemaphoreType.REGULAR((4,)),
        ],
        compiler_params=pltpu.CompilerParams(
            collective_id=0, has_side_effects=True, vmem_limit_bytes=60 * 1024 * 1024
        ),
    )(adjoint, flux_terms, stiffness, normals.transpose(0, 2, 1), design_map.T)
    return lam, grad.reshape(8)


def solution(mesh):
    in_specs = (
        P("inst", None, "space", None, None),
        P("inst", None, None, "space", None, None),
        P("space", "inst", None),
        P(None, "space", "inst"),
        P("space", "inst"),
    )
    out_specs = (P(None, "space", "inst", None), P(("inst", "space")))
    return jax.shard_map(
        per_device, mesh=mesh, in_specs=in_specs, out_specs=out_specs, check_vma=False
    )
```
